32 devices in a mesh: cam: 16 (over z, y, core), frame: 2 (over x).
Axes of the slice: x: 2, y: 2, z: 4, core: 2. Of those that a mesh axis runs over, the one named last changes fastest.
Arguments:
- frames: bfloat16 [16, 64, 3, 4096], P('cam', 'frame'), may hold values from -6 to 6
- conv1_w: bfloat16 [27, 128], replicated, may hold values from -1.25 to 1.25
- conv2_w: bfloat16 [1152, 256], replicated, may hold values from -0.1875 to 0.1875
- tile_w: bfloat16 [256, 128], replicated, may hold values from -0.375 to 0.375
- vis_subject: int32 [16, 64, 12], P('cam', 'frame'), may hold values from 0 to 63, as said below
- part_count: int32 [16, 64, 12], P('cam', 'frame'), may hold values from 6 to 8
- part_region: int32 [16, 64, 12, 8], P('cam', 'frame'), may hold values from 0 to 15
- subject_slot: int32 [64], replicated, may hold values from 0 to 63, as said below
- qkv_w: bfloat16 [1024, 3072], replicated, may hold values from -0.1875 to 0.1875
- out_w: bfloat16 [1024, 1024], replicated, may hold values from -0.1875 to 0.1875
- key_bias: float32 [64, 16, 64], P('cam'), may hold values from -2 to 237
Outputs:
- posed: bfloat16 [64, 64, 1024], P('cam', 'frame')
The draws below stay inside these ranges and needn't reach their ends.
Inputs may be any that keep to these rules, and one draw needn't show every extreme that they name: `vis_subject`: each camera frame lists 12 distinct subjects. Rows of the subject-owned arrays form blocks of 4 (the rows of one index of cam); one list names at most 2 subjects whose rows lie in one block, and for each aligned block of 32 frames one row block, drawn for it, has exactly 2 subjects in every camera's list of every frame of it. `subject_slot`: A permutation of the subjects' numbers.
All inputs are finite; a program needn't handle non-finite values.
Results may differ from the reference program's by a relative error of at most 0.0085.
Values may be sent and summed in bfloat16 or wider, within the bound.
No kernel may reach another device: no remote copies, remote signals or barrier semaphores. Data moves between devices by JAX's collectives and lax.ppermute only.
A program may use at most 64 MiB of HBM per device.

```python
import math
import jax
import jax.numpy as jnp
from jax import lax

IMG = 64
RGRID = 4
REGIONS = 16
C1 = 128
C2 = 256
TILE = 128
PARTS_SIZE = 8
D = 1024
HEADS = 16
FR_DEV = 32
SUBJ_DEV = 4
PER_OWN = 2
VIS = 12
CAMERAS = 16
SUBJECTS = 64
FRAMES = 64
N_CAM = 16
N_FRAME = 2


def visibility_tables(key):
    anchor = jax.random.fold_in(key, 101)
    slot_of = jax.random.permutation(jax.random.fold_in(anchor, 1), SUBJECTS).astype(jnp.int32)
    subject_at = jnp.argsort(slot_of).astype(jnp.int32)
    busy_block = jax.random.randint(jax.random.fold_in(anchor, 2), (N_FRAME,), 0, N_CAM)
    busy_rows = jnp.repeat(busy_block, FR_DEV)
    token_total = N_CAM * PER_OWN
    token_ids = jnp.arange(token_total, dtype=jnp.int32)
    owner_of_token = token_ids // PER_OWN
    raw_scores = jax.random.randint(jax.random.fold_in(anchor, 3), (CAMERAS, FRAMES, token_total), 0, 1 << 20)
    scores = raw_scores * token_total + token_ids[None, None, :]
    is_busy = owner_of_token[None, None, :] == busy_rows[None, :, None]
    scores = jnp.where(is_busy, token_ids[None, None, :] - token_total, scores)
    chosen = jnp.argsort(scores, axis=-1)[:, :, :VIS].astype(jnp.int32)
    owner_index = chosen // PER_OWN
    copy_index = chosen % PER_OWN
    local_scores = jax.random.randint(jax.random.fold_in(anchor, 4), (CAMERAS, FRAMES, N_CAM, SUBJ_DEV), 0, 1 << 20)
    local_scores = local_scores * SUBJ_DEV + jnp.arange(SUBJ_DEV, dtype=jnp.int32)
    local_order = jnp.argsort(local_scores, axis=-1).astype(jnp.int32).reshape(CAMERAS, FRAMES, N_CAM * SUBJ_DEV)
    picked = jnp.take_along_axis(local_order, owner_index * SUBJ_DEV + copy_index, axis=-1)
    slot_rows = owner_index * SUBJ_DEV + picked
    mixing = jax.random.randint(jax.random.fold_in(anchor, 5), (CAMERAS, FRAMES, VIS), 0, 1 << 20)
    mixing = mixing * VIS + jnp.arange(VIS, dtype=jnp.int32)
    shuffle = jnp.argsort(mixing, axis=-1).astype(jnp.int32)
    slot_rows = jnp.take_along_axis(slot_rows, shuffle, axis=-1)
    return (slot_of, subject_at[slot_rows].astype(jnp.int32))


def draw_vis_subject(key, part):
    return visibility_tables(key)[1]


def draw_subject_slot(key, part):
    return visibility_tables(key)[0]


def draw_key_bias(key, part):
    bias_shape = (SUBJECTS, HEADS, FRAMES)
    background = jax.random.uniform(jax.random.fold_in(key, 11), bias_shape, jnp.float32, -2.0, 2.0)
    return background


def set_ends(entries, key, low, high):
    longest = entries.shape.index(max(entries.shape))
    spots = []
    for shift in (0, 1):
        where = [jax.random.randint(jax.random.fold_in(key, axis), (), 0, length) for axis, length in enumerate(entries.shape)]
        where[longest] = (where[longest] + shift) % entries.shape[longest]
        spots.append(tuple(where))
    return entries.at[spots[0]].set(low).at[spots[1]].set(high)


def steps_of(own_key, shape, pieces, least, high):
    factor_of = 1.0
    for dim, parts in pieces:
        draws = jax.random.uniform(jax.random.fold_in(jax.random.fold_in(own_key, 6), dim), (parts,), jnp.float32, least / len(pieces), high / len(pieces))
        factor_of = factor_of * jnp.repeat(jnp.exp(draws), shape[dim] // parts).reshape((-1,) + (1,) * (len(shape) - 1 - dim))
    return factor_of


def centred(stream_key, shape, width, limit, cuts=(), held_as=jnp.bfloat16):
    level = steps_of(stream_key, shape, cuts, -0.22, 0.18) if cuts else 1.0
    entries = jax.random.normal(stream_key, shape, jnp.float32) * width * level
    return jnp.minimum(jnp.maximum(entries, -limit), limit).astype(held_as)


def setup_inputs(seed: int = 0) -> dict:
    key_list = jax.random.split(jax.random.key(seed), 12)
    frames = centred(key_list[0], (CAMERAS, FRAMES, 3, IMG * IMG), 1.0, 6.0, ((0, 16), (1, 2)))
    conv1_w = centred(key_list[1], (27, C1), 27 ** -0.5, 1.25)
    conv2_w = centred(key_list[2], (9 * C1, C2), (9 * C1) ** -0.5, 0.1875)
    tile_w = centred(key_list[3], (C2, TILE), C2 ** -0.5, 0.375)
    vis_subject = draw_vis_subject(jax.random.fold_in(key_list[11], 71), 0)
    part_count = set_ends(jax.random.randint(key_list[5], (CAMERAS, FRAMES, VIS), PARTS_SIZE - PARTS_SIZE // 4, PARTS_SIZE + 1), jax.random.fold_in(key_list[5], 1), PARTS_SIZE - PARTS_SIZE // 4, PARTS_SIZE).astype(jnp.int32)
    part_region = set_ends(jax.random.randint(key_list[6], (CAMERAS, FRAMES, VIS, PARTS_SIZE), 0, REGIONS), jax.random.fold_in(key_list[6], 1), 0, REGIONS - 1).astype(jnp.int32)
    subject_slot = draw_subject_slot(jax.random.fold_in(key_list[11], 71), 0)
    qkv_w = centred(key_list[8], (D, 3 * D), D ** -0.5, 0.1875)
    out_w = centred(key_list[9], (D, D), D ** -0.5, 0.1875)
    key_bias = draw_key_bias(jax.random.fold_in(key_list[11], 71), 0)
    return dict(frames=frames, conv1_w=conv1_w, conv2_w=conv2_w, tile_w=tile_w, vis_subject=vis_subject, part_count=part_count, part_region=part_region, subject_slot=subject_slot, qkv_w=qkv_w, out_w=out_w, key_bias=key_bias)


EPS = 1e-05

def conv_features(pictures, conv1_w, conv2_w):
    amount = pictures.shape[0]
    images = pictures.reshape(amount, 3, IMG, IMG)
    section_one = lax.conv_general_dilated(images, conv1_w.reshape(3, 3, 3, C1), (2, 2), ((1, 1), (1, 1)), dimension_numbers=('NCHW', 'HWIO', 'NHWC'), preferred_element_type=jnp.float32)
    section_one = jax.nn.relu(section_one).astype(jnp.bfloat16)
    section_two = lax.conv_general_dilated(section_one, conv2_w.reshape(3, 3, C1, C2), (2, 2), ((1, 1), (1, 1)), dimension_numbers=('NHWC', 'HWIO', 'NHWC'), preferred_element_type=jnp.float32)
    section_two = jax.nn.relu(section_two)
    patch_side = IMG // (4 * RGRID)
    pooled = lax.optimization_barrier(jnp.mean(section_two.reshape(amount, RGRID, patch_side, RGRID, patch_side, C2), axis=(2, 4)))
    return pooled.reshape(amount, RGRID * RGRID, C2).astype(jnp.bfloat16)

def reference(frames, conv1_w, conv2_w, tile_w, vis_subject, part_count, part_region, subject_slot, qkv_w, out_w, key_bias):

    def camera_tiles(pictures):
        pooled = conv_features(pictures, conv1_w, conv2_w)
        projected = jnp.dot(pooled.reshape(FRAMES * REGIONS, C2), tile_w, preferred_element_type=jnp.float32)
        return projected.astype(jnp.bfloat16).reshape(FRAMES, REGIONS, TILE)
    tiles = lax.map(camera_tiles, frames)
    frame_index = jnp.arange(FRAMES, dtype=jnp.int32)
    part_index = jnp.arange(PARTS_SIZE, dtype=jnp.int32)

    def add_camera(running, inputs):
        tiles_now, listed, counts, regions = inputs
        picked = tiles_now[frame_index[:, None, None], regions]
        visible = part_index[None, None, :] < counts[:, :, None]
        picked = jnp.where(visible[:, :, :, None], picked.astype(jnp.float32), jnp.zeros((), jnp.float32))
        targets = subject_slot[listed] * FRAMES + frame_index[:, None]
        camera_sum = jax.ops.segment_sum(picked.reshape(FRAMES * VIS, D), targets.reshape(FRAMES * VIS), num_segments=SUBJECTS * FRAMES)
        return (running + camera_sum, None)
    tokens = lax.scan(add_camera, jnp.zeros((SUBJECTS * FRAMES, D), jnp.float32), (tiles, vis_subject, part_count, part_region))[0]
    normed = (tokens * lax.rsqrt(lax.optimization_barrier(jnp.mean(tokens * tokens, axis=1, keepdims=True)) + EPS)).astype(jnp.bfloat16)
    mixed = jnp.dot(normed, qkv_w, preferred_element_type=jnp.float32).astype(jnp.bfloat16)
    head_size = D // HEADS
    score_scale = 1.0 / math.sqrt(head_size)
    queries = mixed[:, :D].reshape(SUBJECTS, FRAMES, HEADS, head_size)
    key_rows = mixed[:, D:2 * D].reshape(SUBJECTS, FRAMES, HEADS, head_size)
    value_rows = mixed[:, 2 * D:].reshape(SUBJECTS, FRAMES, HEADS, head_size)

    def attend(inputs):
        query_now, key_now, value_now, bias_now = inputs
        scores = jnp.einsum('qhd,khd->hqk', query_now.astype(jnp.float32), key_now.astype(jnp.float32)) * score_scale
        scores = scores + bias_now[:, None, :]
        row_top = lax.optimization_barrier(jnp.max(scores, axis=2, keepdims=True))
        raw_weights = jnp.exp(scores - row_top)
        denominator = lax.optimization_barrier(jnp.sum(raw_weights, axis=2))
        rounded = lax.optimization_barrier(raw_weights.astype(jnp.bfloat16)).astype(jnp.float32)
        numerator = jnp.einsum('hqk,khd->hqd', rounded, value_now.astype(jnp.float32))
        result = numerator / denominator[:, :, None]
        return jnp.transpose(result, (1, 0, 2)).reshape(FRAMES, D).astype(jnp.bfloat16)
    attended = lax.map(attend, (queries, key_rows, value_rows, key_bias))
    posed = tokens + jnp.dot(attended.reshape(SUBJECTS * FRAMES, D), out_w, preferred_element_type=jnp.float32)
    return posed.astype(jnp.bfloat16).reshape(SUBJECTS, FRAMES, D)
```

```python
import functools
import math

import jax
import jax.numpy as jnp
import numpy as np
from jax import lax
from jax.experimental import pallas as pl
from jax.experimental.pallas import tpu as pltpu
from jax.sharding import PartitionSpec as P

IMG = 64
RGRID = 4
HEADS = 16
SUBJ_DEV = 4
EPS = 1e-05

LANES = 128
BF = jnp.bfloat16
F32 = jnp.float32
OUT1 = IMG // 2
OUT2 = IMG // 4
PATCH = OUT2 // RGRID
REGIONS = RGRID * RGRID
GROUP = 8
GROUPS = OUT1 // GROUP
SEG = 21
VMEM_ALL = pl.BlockSpec(memory_space=pltpu.VMEM)


def pack_table():
    table = np.zeros((3 * LANES, GROUPS * LANES), np.float32)
    for group in range(GROUPS):
        for row in range(2):
            for ch in range(3):
                for pos in range(2 * GROUP + 1):
                    pixel = 2 * GROUP * group - 1 + pos
                    if 0 <= pixel < IMG:
                        source = ch * LANES + row * IMG + pixel
                        table[source, group * LANES + row * IMG + ch * SEG + pos] = 1.0
    return table


def tap_table():
    table = np.zeros((GROUP, 2 * LANES, 32), np.float32)
    for column in range(GROUP):
        for dy in range(3):
            base = {1: 0, 2: IMG, 0: LANES + IMG}[dy]
            for dx in range(3):
                for ch in range(3):
                    lane = base + ch * SEG + 2 * column + dx
                    table[column, lane, dy * 9 + dx * 3 + ch] = 1.0
    return table.reshape(GROUP * 2 * LANES, 32)


def camera_kernel(
    x_ref, pack_ref, tap_ref, w1_ref, w2_ref, wt_ref, vis_ref, count_ref, region_ref, slot_ref,
    out_ref, packed, wide, cells, part, *, subjects, parts
):
    frames_here = x_ref.shape[1]
    rows = OUT1 * frames_here
    listed = vis_ref.shape[1]
    lanes = listed * parts
    expand = (
        lax.broadcasted_iota(jnp.int32, (listed, lanes), 1) // parts
        == lax.broadcasted_iota(jnp.int32, (listed, lanes), 0)
    ).astype(BF)

    def spread(ref):
        return jnp.dot(ref[...].astype(F32).astype(BF), expand, preferred_element_type=F32)

    who = spread(vis_ref).astype(jnp.int32)
    count = spread(count_ref).astype(jnp.int32)
    part_of = lax.broadcasted_iota(jnp.int32, (frames_here, lanes), 1) % parts
    code = jnp.where(part_of < count, region_ref[...] + 1, 0)
    row_of = jnp.zeros((frames_here, lanes), jnp.int32)
    for subject in range(subjects):
        row_of = jnp.where(who == subject, slot_ref[subject], row_of)
    blocks = -(-lanes // LANES)
    fill = blocks * LANES - lanes
    if fill:
        zeros = jnp.zeros((frames_here, fill), jnp.int32)
        code = jnp.concatenate([code, zeros], axis=1)
        row_of = jnp.concatenate([row_of, zeros], axis=1)
    base = REGIONS * frames_here
    for k, array in enumerate((code, row_of)):
        for block in range(blocks):
            at = base + (k * blocks + block) * frames_here
            out_ref[at : at + frames_here, :] = (
                array[:, block * LANES : (block + 1) * LANES].astype(F32).astype(BF)
            )

    for column in range(GROUP):
        wide[:, column * LANES : (column + 1) * LANES] = jnp.dot(
            tap_ref[column * 2 * LANES : (column + 1) * 2 * LANES, :],
            w1_ref[...],
            preferred_element_type=F32,
        ).astype(BF)
    packed[:, 0:frames_here, :] = jnp.zeros((GROUPS, frames_here, LANES), BF)
    images = jnp.concatenate(
        [
            jnp.concatenate(
                [x_ref[ch, :, y * LANES : (y + 1) * LANES] for ch in range(3)], axis=1
            )
            for y in range(OUT1)
        ],
        axis=0,
    )
    for group in range(GROUPS):
        packed[group, frames_here:, :] = jnp.dot(
            images, pack_ref[:, group * LANES : (group + 1) * LANES], preferred_element_type=F32
        ).astype(BF)
    cells[0] = jnp.zeros(cells.shape[1:], BF)
    cells[:, 1, 0] = jnp.zeros((cells.shape[0],) + cells.shape[3:], BF)
    for group in range(GROUPS):
        lhs = jnp.concatenate(
            [packed[group, frames_here:, :], packed[group, 0:rows, :]], axis=1
        )
        for pair in range(GROUP // 2):
            both = jnp.dot(
                lhs, wide[:, pair * 2 * LANES : (pair + 1) * 2 * LANES], preferred_element_type=F32
            )
            both = jnp.maximum(both, 0.0).astype(BF)
            at = group * (GROUP // 2) + pair
            cells[1:, 0, at] = both[:, :LANES].reshape(OUT1, frames_here, LANES)
            cells[1:, 1, at + 1] = both[:, LANES:].reshape(OUT1, frames_here, LANES)

    width = w2_ref.shape[1]
    for ry in range(RGRID):
        total = jnp.zeros((RGRID, frames_here, width), F32)
        for y in range(ry * PATCH, (ry + 1) * PATCH):
            taps = []
            for dy in range(3):
                for parity, start in ((1, 0), (0, 0), (1, 1)):
                    taps.append(
                        cells[2 * y + dy, parity, start : start + OUT2].reshape(
                            OUT2 * frames_here, LANES
                        )
                    )
            two = jnp.dot(
                jnp.concatenate(taps, axis=1), w2_ref[...], preferred_element_type=F32
            )
            two = jnp.maximum(two, 0.0).reshape(RGRID, PATCH, frames_here, width)
            for k in range(PATCH):
                total = total + two[:, k]
        pooled = (total * (1.0 / (PATCH * PATCH))).astype(BF)
        tiles = jnp.dot(
            pooled.reshape(RGRID * frames_here, width), wt_ref[...], preferred_element_type=F32
        )
        for rx in range(RGRID):
            part[pl.ds(ry * RGRID + rx, frames_here, stride=REGIONS), :] = tiles[
                rx * frames_here : (rx + 1) * frames_here
            ]
    out_ref[0:base, :] = part[...].astype(BF)


def camera_tiles(frames, conv1_w, conv2_w, tile_w, vis_subject, part_count, part_region, slots):
    frames_here = frames.shape[1]
    listed, parts = part_region.shape[2:]
    blocks = -(-listed * parts // LANES)
    images = jnp.transpose(frames[0], (1, 0, 2))
    taps = jnp.pad(conv1_w, ((0, 32 - conv1_w.shape[0]), (0, 0)))
    return pl.pallas_call(
        functools.partial(camera_kernel, subjects=slots.shape[0], parts=parts),
        out_shape=jax.ShapeDtypeStruct(((REGIONS + 2 * blocks) * frames_here, LANES), BF),
        in_specs=[VMEM_ALL] * 9 + [pl.BlockSpec(memory_space=pltpu.SMEM)],
        out_specs=VMEM_ALL,
        scratch_shapes=[
            pltpu.VMEM((GROUPS, (OUT1 + 1) * frames_here, LANES), BF),
            pltpu.VMEM((2 * LANES, GROUP * LANES), BF),
            pltpu.VMEM((OUT1 + 1, 2, OUT2 + 1, frames_here, LANES), BF),
            pltpu.VMEM((REGIONS * frames_here, LANES), F32),
        ],
        compiler_params=pltpu.CompilerParams(vmem_limit_bytes=50 << 20),
    )(
        images,
        jnp.asarray(pack_table(), BF),
        jnp.asarray(tap_table(), BF),
        taps,
        conv2_w,
        tile_w,
        vis_subject[0],
        part_count[0],
        part_region[0].reshape(frames_here, listed * parts),
        slots,
    )


def exchange(payload):
    cams = lax.axis_size("cam")
    if cams & (cams - 1):
        gathered = lax.all_gather(payload, "cam", axis=0, tiled=False)
        return [gathered[c] for c in range(cams)]

    def swap(array, bits):
        return lax.ppermute(array, "cam", [(i, i ^ bits) for i in range(cams)])

    pieces = [payload] + [swap(payload, bits) for bits in range(2, cams, 2)]
    return pieces + [swap(piece, 1) for piece in pieces]


def token_kernel(me_ref, *refs, cams, parts, frames_here):
    pieces = refs[:cams]
    tokens_ref, normed_ref, marks, spots, picks, summed = refs[cams:]
    blocks = (pieces[0].shape[0] // frames_here - REGIONS) // 2
    lanes = blocks * LANES
    places = SUBJ_DEV * parts
    first = me_ref[0] * SUBJ_DEV
    base = REGIONS * frames_here
    from_lane = lax.broadcasted_iota(jnp.int32, (SUBJ_DEV * lanes, LANES), 0)
    to_lane = lax.broadcasted_iota(jnp.int32, (SUBJ_DEV * lanes, LANES), 1)
    fold = (
        (from_lane % parts == to_lane % parts) & (from_lane // lanes == to_lane // parts)
    ).astype(BF)
    codes = []
    for piece in pieces:

        def field(k):
            return jnp.concatenate(
                [
                    piece[
                        base + (k * blocks + b) * frames_here : base
                        + (k * blocks + b + 1) * frames_here,
                        :,
                    ].astype(F32)
                    for b in range(blocks)
                ],
                axis=1,
            )

        code, row = field(0), field(1)
        codes.append(
            jnp.concatenate(
                [
                    jnp.where(row == (first + s).astype(F32), code, 0.0).astype(BF)
                    for s in range(SUBJ_DEV)
                ],
                axis=1,
            )
        )
    marks[...] = jnp.dot(jnp.concatenate(codes, axis=0), fold, preferred_element_type=F32)
    for f in range(frames_here):
        found = marks[pl.ds(f, cams, stride=frames_here), :]
        spots[f * places : (f + 1) * places, :] = found.T[:places].astype(BF)
    widen = (
        lax.broadcasted_iota(jnp.int32, (cams, cams * REGIONS), 1) // REGIONS
        == lax.broadcasted_iota(jnp.int32, (cams, cams * REGIONS), 0)
    ).astype(BF)
    spread = jnp.dot(spots[...], widen, preferred_element_type=F32)
    region = lax.broadcasted_iota(jnp.int32, spread.shape, 1) % REGIONS + 1
    picks[...] = jnp.where(spread == region.astype(F32), 1.0, 0.0).astype(BF)
    for f in range(frames_here):
        tiles = jnp.concatenate(
            [piece[f * REGIONS : (f + 1) * REGIONS, :] for piece in pieces], axis=0
        )
        summed[f * places : (f + 1) * places, :] = jnp.dot(
            picks[f * places : (f + 1) * places, :], tiles, preferred_element_type=F32
        )
    for s in range(SUBJ_DEV):
        tokens = jnp.concatenate(
            [
                summed[pl.ds(s * parts + p, frames_here, stride=places), :]
                for p in range(parts)
            ],
            axis=1,
        )
        tokens_ref[s * frames_here : (s + 1) * frames_here, :] = tokens
        power = jnp.mean(tokens * tokens, axis=1, keepdims=True)
        normed_ref[s * frames_here : (s + 1) * frames_here, :] = (
            tokens * lax.rsqrt(power + EPS)
        ).astype(BF)


def build_tokens(pieces, parts, frames_here):
    cams = len(pieces)
    rows = SUBJ_DEV * frames_here
    width = parts * LANES
    places = SUBJ_DEV * parts
    me = lax.axis_index("cam").astype(jnp.int32).reshape(1)
    return pl.pallas_call(
        functools.partial(token_kernel, cams=cams, parts=parts, frames_here=frames_here),
        out_shape=(
            jax.ShapeDtypeStruct((rows, width), F32),
            jax.ShapeDtypeStruct((rows, width), BF),
        ),
        in_specs=[pl.BlockSpec(memory_space=pltpu.SMEM)] + [VMEM_ALL] * cams,
        out_specs=(VMEM_ALL, VMEM_ALL),
        scratch_shapes=[
            pltpu.VMEM((cams * frames_here, LANES), F32),
            pltpu.VMEM((frames_here * places, cams), BF),
            pltpu.VMEM((frames_here * places, cams * REGIONS), BF),
            pltpu.VMEM((frames_here * places, LANES), F32),
        ],
        compiler_params=pltpu.CompilerParams(vmem_limit_bytes=50 << 20),
    )(me, *pieces)


def attention_kernel(
    mixed_ref, other_ref, key_w_ref, value_w_ref, out_w_ref, bias_ref, tokens_ref,
    out_ref, other_keys, other_values, attended, *, frames_here
):
    rows, width = tokens_ref.shape
    others = other_ref.shape[0] // rows
    head_size = width // HEADS
    scale = 1.0 / math.sqrt(head_size)
    other_keys[...] = jnp.dot(
        other_ref[...], key_w_ref[...], preferred_element_type=F32
    ).astype(BF)
    other_values[...] = jnp.dot(
        other_ref[...], value_w_ref[...], preferred_element_type=F32
    ).astype(BF)
    span = (others + 1) * frames_here
    heads = LANES // head_size
    head_of = lax.broadcasted_iota(jnp.int32, (frames_here, LANES), 1) // head_size
    for n in range(SUBJ_DEV):
        at = n * frames_here
        for tile in range(width // LANES):
            lanes = slice(tile * LANES, (tile + 1) * LANES)

            def gathered(own, rest):
                return jnp.concatenate(
                    [mixed_ref[at : at + frames_here, own + tile * LANES : own + (tile + 1) * LANES]]
                    + [
                        rest[k * rows + at : k * rows + at + frames_here, lanes]
                        for k in range(others)
                    ],
                    axis=0,
                )

            query = mixed_ref[at : at + frames_here, lanes]
            queries = jnp.concatenate(
                [jnp.where(head_of == h, query, jnp.zeros((), BF)) for h in range(heads)], axis=0
            )
            scores = lax.dot_general(
                queries,
                gathered(width, other_keys),
                (((1,), (1,)), ((), ())),
                preferred_element_type=F32,
            )
            bias = jnp.concatenate(
                [
                    jnp.broadcast_to(
                        bias_ref[n, tile * heads + h : tile * heads + h + 1, :],
                        (frames_here, span),
                    )
                    for h in range(heads)
                ],
                axis=0,
            )
            scores = scores * scale + bias
            weights = jnp.exp(scores - jnp.max(scores, axis=1, keepdims=True))
            denominator = jnp.sum(weights, axis=1, keepdims=True)
            numerator = jnp.dot(
                weights.astype(BF), gathered(2 * width, other_values), preferred_element_type=F32
            )
            ratio = numerator / denominator
            result = ratio[:frames_here]
            for h in range(1, heads):
                result = jnp.where(
                    head_of == h, ratio[h * frames_here : (h + 1) * frames_here], result
                )
            attended[at : at + frames_here, lanes] = result.astype(BF)
    out_ref[...] = (
        tokens_ref[...] + jnp.dot(attended[...], out_w_ref[...], preferred_element_type=F32)
    ).astype(BF)


def attend(mixed, other, qkv_w, out_w, bias, tokens, frames_here):
    rows, width = tokens.shape
    whole = lambda array: pl.BlockSpec(array.shape, lambda i: (0,) * array.ndim)
    return pl.pallas_call(
        functools.partial(attention_kernel, frames_here=frames_here),
        grid=(1,),
        out_shape=jax.ShapeDtypeStruct((rows, width), BF),
        in_specs=[
            whole(mixed),
            whole(other),
            pl.BlockSpec((width, width), lambda i: (0, 1)),
            pl.BlockSpec((width, width), lambda i: (0, 2)),
            whole(out_w),
            whole(bias),
            whole(tokens),
        ],
        out_specs=whole(tokens),
        scratch_shapes=[
            pltpu.VMEM(other.shape, BF),
            pltpu.VMEM(other.shape, BF),
            pltpu.VMEM((rows, width), BF),
        ],
        compiler_params=pltpu.CompilerParams(vmem_limit_bytes=56 << 20),
    )(mixed, other, qkv_w, qkv_w, out_w, bias, tokens)


def per_device(
    frames, conv1_w, conv2_w, tile_w, vis_subject, part_count, part_region, subject_slot,
    qkv_w, out_w, key_bias
):
    frames_here = frames.shape[1]
    parts = part_region.shape[3]
    payload = camera_tiles(
        frames, conv1_w, conv2_w, tile_w, vis_subject, part_count, part_region, subject_slot
    )
    tokens, normed = build_tokens(exchange(payload), parts, frames_here)
    splits = lax.axis_size("frame")
    others = [
        lax.ppermute(normed, "frame", [((i + k) % splits, i) for i in range(splits)])
        for k in range(1, splits)
    ]
    other = others[0] if splits == 2 else jnp.concatenate(others, axis=0)
    mixed = jnp.dot(normed, qkv_w, preferred_element_type=F32).astype(BF)
    span = key_bias.shape[2]
    bias = lax.dynamic_slice_in_dim(
        jnp.concatenate([key_bias, key_bias], axis=2),
        lax.axis_index("frame") * frames_here,
        span,
        axis=2,
    )
    posed = attend(mixed, other, qkv_w, out_w, bias, tokens, frames_here)
    return posed.reshape(SUBJ_DEV, frames_here, tokens.shape[1])


def solution(mesh):
    in_specs = (
        P("cam", "frame", None, None),
        P(),
        P(),
        P(),
        P("cam", "frame", None),
        P("cam", "frame", None),
        P("cam", "frame", None, None),
        P(),
        P(),
        P(),
        P("cam", None, None),
    )
    out_specs = P("cam", "frame", None)
    return jax.shard_map(
        per_device, mesh=mesh, in_specs=in_specs, out_specs=out_specs, check_vma=False
    )
```

```python
import functools
import math

import jax
import jax.numpy as jnp
import numpy as np
from jax import lax
from jax.experimental import pallas as pl
from jax.experimental.pallas import tpu as pltpu
from jax.sharding import PartitionSpec as P

IMG = 64
RGRID = 4
HEADS = 16
SUBJ_DEV = 4
EPS = 1e-05

LANES = 128
BF = jnp.bfloat16
F32 = jnp.float32
OUT1 = IMG // 2
OUT2 = IMG // 4
PATCH = OUT2 // RGRID
REGIONS = RGRID * RGRID
GROUP = 8
GROUPS = OUT1 // GROUP
SEG = 21
VMEM_ALL = pl.BlockSpec(memory_space=pltpu.VMEM)


def pack_table():
    table = np.zeros((3 * LANES, GROUPS * LANES), np.float32)
    for group in range(GROUPS):
        for row in range(2):
            for ch in range(3):
                for pos in range(2 * GROUP + 1):
                    pixel = 2 * GROUP * group - 1 + pos
                    if 0 <= pixel < IMG:
                        source = ch * LANES + row * IMG + pixel
                        table[source, group * LANES + row * IMG + ch * SEG + pos] = 1.0
    return table


def tap_table():
    table = np.zeros((GROUP, 2 * LANES, 27), np.float32)
    for column in range(GROUP):
        for dy in range(3):
            base = {1: 0, 2: IMG, 0: LANES + IMG}[dy]
            for dx in range(3):
                for ch in range(3):
                    lane = base + ch * SEG + 2 * column + dx
                    table[column, lane, dy * 9 + dx * 3 + ch] = 1.0
    return table.reshape(GROUP * 2 * LANES, 27)


def camera_kernel(
    x_hbm, pack_hbm, tap_hbm, w1_hbm, w2_hbm, wt_hbm, vis_hbm, count_hbm, region_hbm, slot_hbm,
    out_ref, x_ref, pack_ref, tap_ref, w1_ref, w2_ref, wt_ref, vis_ref, count_ref, region_ref,
    slot_ref, sems, packed, wide, cells, part, *, subjects, parts
):
    sources = (
        slot_hbm, vis_hbm, count_hbm, region_hbm, w1_hbm, tap_hbm, pack_hbm, x_hbm, w2_hbm, wt_hbm
    )
    targets = (
        slot_ref, vis_ref, count_ref, region_ref, w1_ref, tap_ref, pack_ref, x_ref, w2_ref, wt_ref
    )
    copies = [
        pltpu.make_async_copy(source, target, sems.at[k])
        for k, (source, target) in enumerate(zip(sources, targets))
    ]
    for copy in copies:
        copy.start()
    frames_here = x_ref.shape[1]
    rows = OUT1 * frames_here
    listed = vis_ref.shape[0]
    lanes = listed * parts
    expand = (
        lax.broadcasted_iota(jnp.int32, (lanes, listed), 0) // parts
        == lax.broadcasted_iota(jnp.int32, (lanes, listed), 1)
    ).astype(BF)
    part_of = lax.broadcasted_iota(jnp.int32, (lanes, frames_here), 0) % parts

    for copy in copies[:6]:
        copy.wait()
    for column in range(GROUP):
        wide[:, column * LANES : (column + 1) * LANES] = jnp.dot(
            tap_ref[column * 2 * LANES : (column + 1) * 2 * LANES, :],
            w1_ref[...],
            preferred_element_type=F32,
        ).astype(BF)

    def spread(ref):
        return jnp.dot(
            expand, ref[:, 0, :].astype(F32).astype(BF), preferred_element_type=F32
        ).astype(jnp.int32)

    who = spread(vis_ref)
    code = jnp.where(part_of < spread(count_ref), region_ref[...] + 1, 0)
    row_of = jnp.zeros((lanes, frames_here), jnp.int32)
    for subject in range(subjects):
        row_of = jnp.where(who == subject, slot_ref[subject], row_of)
    blocks = -(-lanes // LANES)
    fill = blocks * LANES - lanes
    base = REGIONS * frames_here
    for k, array in enumerate((code, row_of)):
        array = array.astype(F32)
        if fill:
            array = jnp.concatenate([array, jnp.zeros((fill, frames_here), F32)], axis=0)
        array = array.T.astype(BF)
        for block in range(blocks):
            at = base + (k * blocks + block) * frames_here
            out_ref[at : at + frames_here, :] = array[:, block * LANES : (block + 1) * LANES]

    cells[0] = jnp.zeros(cells.shape[1:], BF)
    cells[:, 1, 0] = jnp.zeros((cells.shape[0],) + cells.shape[3:], BF)
    packed[:, 0:frames_here, :] = jnp.zeros((GROUPS, frames_here, LANES), BF)
    copies[6].wait()
    copies[7].wait()
    images = jnp.concatenate(
        [
            jnp.concatenate(
                [x_ref[ch, :, y * LANES : (y + 1) * LANES] for ch in range(3)], axis=1
            )
            for y in range(OUT1)
        ],
        axis=0,
    )
    for group in range(GROUPS):
        packed[group, frames_here:, :] = jnp.dot(
            images, pack_ref[:, group * LANES : (group + 1) * LANES], preferred_element_type=F32
        ).astype(BF)
    for group in range(GROUPS):
        lhs = jnp.concatenate(
            [packed[group, frames_here:, :], packed[group, 0:rows, :]], axis=1
        )
        for pair in range(GROUP // 2):
            both = jnp.dot(
                lhs, wide[:, pair * 2 * LANES : (pair + 1) * 2 * LANES], preferred_element_type=F32
            )
            both = jnp.maximum(both, 0.0).astype(BF)
            at = group * (GROUP // 2) + pair
            cells[1:, 0, at] = both[:, :LANES].reshape(OUT1, frames_here, LANES)
            cells[1:, 1, at + 1] = both[:, LANES:].reshape(OUT1, frames_here, LANES)

    copies[8].wait()
    copies[9].wait()
    width = w2_ref.shape[1]
    for ry in range(RGRID):
        total = jnp.zeros((RGRID, frames_here, width), F32)
        for y in range(ry * PATCH, (ry + 1) * PATCH):
            taps = []
            for dy in range(3):
                for parity, start in ((1, 0), (0, 0), (1, 1)):
                    taps.append(
                        cells[2 * y + dy, parity, start : start + OUT2].reshape(
                            OUT2 * frames_here, LANES
                        )
                    )
            two = jnp.dot(
                jnp.concatenate(taps, axis=1), w2_ref[...], preferred_element_type=F32
            )
            two = jnp.maximum(two, 0.0).reshape(RGRID, PATCH, frames_here, width)
            for k in range(PATCH):
                total = total + two[:, k]
        pooled = (total * (1.0 / (PATCH * PATCH))).astype(BF)
        tiles = jnp.dot(
            pooled.reshape(RGRID * frames_here, width), wt_ref[...], preferred_element_type=F32
        )
        for rx in range(RGRID):
            part[pl.ds(ry * RGRID + rx, frames_here, stride=REGIONS), :] = tiles[
                rx * frames_here : (rx + 1) * frames_here
            ]
    out_ref[0:base, :] = part[...].astype(BF)


def camera_tiles(frames, conv1_w, conv2_w, tile_w, vis_subject, part_count, part_region, slots):
    frames_here = frames.shape[1]
    listed, parts = part_region.shape[2:]
    blocks = -(-listed * parts // LANES)
    operands = (
        jnp.transpose(frames[0], (1, 0, 2)),
        jnp.asarray(pack_table(), BF),
        jnp.asarray(tap_table(), BF),
        conv1_w,
        conv2_w,
        tile_w,
        jnp.transpose(vis_subject, (2, 0, 1)),
        jnp.transpose(part_count, (2, 0, 1)),
        jnp.transpose(part_region[0], (1, 2, 0)).reshape(listed * parts, frames_here),
        slots,
    )
    return pl.pallas_call(
        functools.partial(camera_kernel, subjects=slots.shape[0], parts=parts),
        out_shape=jax.ShapeDtypeStruct(((REGIONS + 2 * blocks) * frames_here, LANES), BF),
        in_specs=[pl.BlockSpec(memory_space=pltpu.HBM)] * len(operands),
        out_specs=VMEM_ALL,
        scratch_shapes=[pltpu.VMEM(array.shape, array.dtype) for array in operands[:-1]]
        + [
            pltpu.SMEM(slots.shape, slots.dtype),
            pltpu.SemaphoreType.DMA((len(operands),)),
            pltpu.VMEM((GROUPS, (OUT1 + 1) * frames_here, LANES), BF),
            pltpu.VMEM((2 * LANES, GROUP * LANES), BF),
            pltpu.VMEM((OUT1 + 1, 2, OUT2 + 1, frames_here, LANES), BF),
            pltpu.VMEM((REGIONS * frames_here, LANES), F32),
        ],
        compiler_params=pltpu.CompilerParams(vmem_limit_bytes=60 << 20),
    )(*operands)


def exchange(payload):
    cams = lax.axis_size("cam")
    if cams & (cams - 1):
        gathered = lax.all_gather(payload, "cam", axis=0, tiled=False)
        return [gathered[c] for c in range(cams)]

    def swap(array, bits):
        return lax.ppermute(array, "cam", [(i, i ^ bits) for i in range(cams)])

    pieces = [payload] + [swap(payload, bits) for bits in range(2, cams, 2)]
    return pieces + [swap(piece, 1) for piece in pieces]


def token_kernel(*refs, cams, parts, frames_here):
    tokens_ref, normed_ref, own, sem, marks, spots, picks, summed = refs[cams:]
    copy = pltpu.make_async_copy(refs[0], own, sem)
    copy.start()
    pieces = refs[1:cams] + (own,)
    blocks = (pieces[0].shape[0] // frames_here - REGIONS) // 2
    lanes = blocks * LANES
    places = SUBJ_DEV * parts
    first = lax.axis_index("cam") * SUBJ_DEV
    base = REGIONS * frames_here
    from_lane = lax.broadcasted_iota(jnp.int32, (SUBJ_DEV * lanes, LANES), 0)
    to_lane = lax.broadcasted_iota(jnp.int32, (SUBJ_DEV * lanes, LANES), 1)
    fold = (
        (from_lane % parts == to_lane % parts) & (from_lane // lanes == to_lane // parts)
    ).astype(BF)
    codes = []
    for piece in pieces:
        if piece is own:
            copy.wait()

        def field(k):
            return jnp.concatenate(
                [
                    piece[
                        base + (k * blocks + b) * frames_here : base
                        + (k * blocks + b + 1) * frames_here,
                        :,
                    ].astype(F32)
                    for b in range(blocks)
                ],
                axis=1,
            )

        code, row = field(0), field(1)
        codes.append(
            jnp.concatenate(
                [
                    jnp.where(row == (first + s).astype(F32), code, 0.0).astype(BF)
                    for s in range(SUBJ_DEV)
                ],
                axis=1,
            )
        )
    marks[...] = jnp.dot(jnp.concatenate(codes, axis=0), fold, preferred_element_type=F32)
    for f in range(frames_here):
        found = marks[pl.ds(f, cams, stride=frames_here), :]
        spots[f * places : (f + 1) * places, :] = found.T[:places].astype(BF)
    widen = (
        lax.broadcasted_iota(jnp.int32, (cams, cams * REGIONS), 1) // REGIONS
        == lax.broadcasted_iota(jnp.int32, (cams, cams * REGIONS), 0)
    ).astype(BF)
    spread = jnp.dot(spots[...], widen, preferred_element_type=F32)
    region = lax.broadcasted_iota(jnp.int32, spread.shape, 1) % REGIONS + 1
    picks[...] = jnp.where(spread == region.astype(F32), 1.0, 0.0).astype(BF)
    for f in range(frames_here):
        tiles = jnp.concatenate(
            [piece[f * REGIONS : (f + 1) * REGIONS, :] for piece in pieces], axis=0
        )
        summed[f * places : (f + 1) * places, :] = jnp.dot(
            picks[f * places : (f + 1) * places, :], tiles, preferred_element_type=F32
        )
    for s in range(SUBJ_DEV):
        tokens = jnp.concatenate(
            [
                summed[pl.ds(s * parts + p, frames_here, stride=places), :]
                for p in range(parts)
            ],
            axis=1,
        )
        tokens_ref[s * frames_here : (s + 1) * frames_here, :] = tokens
        power = jnp.mean(tokens * tokens, axis=1, keepdims=True)
        normed_ref[s * frames_here : (s + 1) * frames_here, :] = (
            tokens * lax.rsqrt(power + EPS)
        ).astype(BF)


def build_tokens(pieces, parts, frames_here):
    cams = len(pieces)
    rows = SUBJ_DEV * frames_here
    width = parts * LANES
    places = SUBJ_DEV * parts
    return pl.pallas_call(
        functools.partial(token_kernel, cams=cams, parts=parts, frames_here=frames_here),
        out_shape=(
            jax.ShapeDtypeStruct((rows, width), F32),
            jax.ShapeDtypeStruct((rows, width), BF),
        ),
        in_specs=[pl.BlockSpec(memory_space=pl.ANY)] + [VMEM_ALL] * (cams - 1),
        out_specs=(VMEM_ALL, VMEM_ALL),
        scratch_shapes=[
            pltpu.VMEM(pieces[0].shape, BF),
            pltpu.SemaphoreType.DMA,
            pltpu.VMEM((cams * frames_here, LANES), F32),
            pltpu.VMEM((frames_here * places, cams), BF),
            pltpu.VMEM((frames_here * places, cams * REGIONS), BF),
            pltpu.VMEM((frames_here * places, LANES), F32),
        ],
        compiler_params=pltpu.CompilerParams(vmem_limit_bytes=10 << 20),
    )(*pieces)


def project_kernel(
    normed_ref, qkv_w_hbm, mixed_ref, key_w_ref, value_w_ref, query_w_ref, sems
):
    width = normed_ref.shape[1]
    half = width // 2
    targets = (query_w_ref, key_w_ref, value_w_ref)
    pieces = [(target, k, at) for k, target in enumerate(targets) for at in (0, half)]
    copies = [
        pltpu.make_async_copy(
            qkv_w_hbm.at[:, pl.ds(k * width + at, half)], target.at[:, pl.ds(at, half)], sems.at[n]
        )
        for n, (target, k, at) in enumerate(pieces)
    ]
    for copy in copies:
        copy.start()
    for copy, (target, k, at) in zip(copies, pieces):
        copy.wait()
        mixed_ref[:, k * width + at : k * width + at + half] = jnp.dot(
            normed_ref[...], target[:, at : at + half], preferred_element_type=F32
        ).astype(BF)


def project(normed, qkv_w):
    rows, width = normed.shape
    hbm = pl.BlockSpec(memory_space=pltpu.HBM)
    square = jax.ShapeDtypeStruct((width, width), BF)
    return pl.pallas_call(
        project_kernel,
        out_shape=[jax.ShapeDtypeStruct((rows, 3 * width), BF), square, square],
        in_specs=[VMEM_ALL, hbm],
        out_specs=[VMEM_ALL] * 3,
        scratch_shapes=[pltpu.VMEM((width, width), BF), pltpu.SemaphoreType.DMA((6,))],
        cost_estimate=pl.CostEstimate(
            flops=2 * rows * width * 3 * width,
            bytes_accessed=2 * qkv_w.size,
            transcendentals=0,
        ),
        compiler_params=pltpu.CompilerParams(vmem_limit_bytes=47 << 20),
    )(normed, qkv_w)


def attention_kernel(
    mixed_ref, other_ref, key_w_ref, value_w_ref, tokens_ref, out_w_hbm, bias_hbm,
    out_ref, out_w_ref, bias_ref, sems, other_keys, other_values, scores, weights, totals, attended, *, frames_here
):
    rows, width = tokens_ref.shape
    others = other_ref.shape[0] // rows
    head_size = width // HEADS
    scale = 1.0 / math.sqrt(head_size)
    splits = others + 1
    span = splits * frames_here
    heads = LANES // head_size
    block = heads * frames_here
    tiles = width // LANES
    head_of = lax.broadcasted_iota(jnp.int32, (frames_here, LANES), 1) // head_size
    place = lax.axis_index("frame")
    copies = [
        pltpu.make_async_copy(source, target, sems.at[k])
        for k, (source, target) in enumerate(((bias_hbm, bias_ref), (out_w_hbm, out_w_ref)))
    ]
    for copy in copies:
        copy.start()
    other_keys[...] = jnp.dot(
        other_ref[...], key_w_ref[...], preferred_element_type=F32
    ).astype(BF)
    other_values[...] = jnp.dot(
        other_ref[...], value_w_ref[...], preferred_element_type=F32
    ).astype(BF)

    def gathered(n, tile, own, rest):
        at = n * frames_here
        return jnp.concatenate(
            [mixed_ref[at : at + frames_here, own + tile * LANES : own + (tile + 1) * LANES]]
            + [
                rest[k * rows + at : k * rows + at + frames_here, tile * LANES : (tile + 1) * LANES]
                for k in range(others)
            ],
            axis=0,
        )

    copies[0].wait()
    for n in range(SUBJ_DEV):
        bias = bias_ref[n]
        turned = bias
        for k in range(1, splits):
            turn = jnp.concatenate(
                [bias[:, k * frames_here :], bias[:, : k * frames_here]], axis=1
            )
            turned = jnp.where(place == k, turn, turned)
        for tile in range(tiles):
            query = mixed_ref[
                n * frames_here : (n + 1) * frames_here, tile * LANES : (tile + 1) * LANES
            ]
            queries = jnp.concatenate(
                [jnp.where(head_of == h, query, jnp.zeros((), BF)) for h in range(heads)], axis=0
            )
            products = lax.dot_general(
                queries,
                gathered(n, tile, width, other_keys),
                (((1,), (1,)), ((), ())),
                preferred_element_type=F32,
            )
            added = jnp.concatenate(
                [
                    jnp.broadcast_to(
                        turned[tile * heads + h : tile * heads + h + 1, :], (frames_here, span)
                    )
                    for h in range(heads)
                ],
                axis=0,
            )
            at = (n * tiles + tile) * block
            scores[at : at + block, :] = products * scale + added
    for n in range(SUBJ_DEV):
        part = slice(n * tiles * block, (n + 1) * tiles * block)
        raw = scores[part, :]
        raised = jnp.exp(raw - jnp.max(raw, axis=1, keepdims=True))
        weights[part, :] = raised.astype(BF)
        totals[part, :] = jnp.broadcast_to(
            jnp.sum(raised, axis=1, keepdims=True), (tiles * block, LANES)
        )
    for n in range(SUBJ_DEV):
        for tile in range(tiles):
            at = (n * tiles + tile) * block
            ratio = (
                jnp.dot(
                    weights[at : at + block, :],
                    gathered(n, tile, 2 * width, other_values),
                    preferred_element_type=F32,
                )
                / totals[at : at + block, :]
            )
            result = ratio[:frames_here]
            for h in range(1, heads):
                result = jnp.where(
                    head_of == h, ratio[h * frames_here : (h + 1) * frames_here], result
                )
            attended[
                n * frames_here : (n + 1) * frames_here, tile * LANES : (tile + 1) * LANES
            ] = result.astype(BF)
    copies[1].wait()
    out_ref[...] = (
        tokens_ref[...] + jnp.dot(attended[...], out_w_ref[...], preferred_element_type=F32)
    ).astype(BF)


def attend(mixed, other, key_w, value_w, out_w, bias, tokens, frames_here):
    rows, width = tokens.shape
    span = bias.shape[2]
    return pl.pallas_call(
        functools.partial(attention_kernel, frames_here=frames_here),
        out_shape=jax.ShapeDtypeStruct((rows, width), BF),
        in_specs=[VMEM_ALL] * 5 + [pl.BlockSpec(memory_space=pltpu.HBM)] * 2,
        out_specs=VMEM_ALL,
        scratch_shapes=[
            pltpu.VMEM(out_w.shape, BF),
            pltpu.VMEM(bias.shape, F32),
            pltpu.SemaphoreType.DMA((2,)),
            pltpu.VMEM(other.shape, BF),
            pltpu.VMEM(other.shape, BF),
            pltpu.VMEM((HEADS * rows, span), F32),
            pltpu.VMEM((HEADS * rows, span), BF),
            pltpu.VMEM((HEADS * rows, LANES), F32),
            pltpu.VMEM((rows, width), BF),
        ],
        compiler_params=pltpu.CompilerParams(vmem_limit_bytes=14 << 20),
    )(mixed, other, key_w, value_w, tokens, out_w, bias)


def per_device(
    frames, conv1_w, conv2_w, tile_w, vis_subject, part_count, part_region, subject_slot,
    qkv_w, out_w, key_bias
):
    frames_here = frames.shape[1]
    parts = part_region.shape[3]
    payload = camera_tiles(
        frames, conv1_w, conv2_w, tile_w, vis_subject, part_count, part_region, subject_slot
    )
    tokens, normed = build_tokens(exchange(payload), parts, frames_here)
    splits = lax.axis_size("frame")
    others = [
        lax.ppermute(normed, "frame", [((i + k) % splits, i) for i in range(splits)])
        for k in range(1, splits)
    ]
    other = others[0] if splits == 2 else jnp.concatenate(others, axis=0)
    mixed, key_w, value_w = project(normed, qkv_w)
    posed = attend(mixed, other, key_w, value_w, out_w, key_bias, tokens, frames_here)
    return posed.reshape(SUBJ_DEV, frames_here, tokens.shape[1])


def solution(mesh):
    in_specs = (
        P("cam", "frame", None, None),
        P(),
        P(),
        P(),
        P("cam", "frame", None),
        P("cam", "frame", None),
        P("cam", "frame", None, None),
        P(),
        P(),
        P(),
        P("cam", None, None),
    )
    out_specs = P("cam", "frame", None)
    return jax.shard_map(
        per_device, mesh=mesh, in_specs=in_specs, out_specs=out_specs, check_vma=False
    )
```

```python
import functools
import math

import jax
import jax.numpy as jnp
import numpy as np
from jax import lax
from jax.experimental import pallas as pl
from jax.experimental.pallas import tpu as pltpu
from jax.sharding import PartitionSpec as P

IMG = 64
RGRID = 4
HEADS = 16
SUBJ_DEV = 4
EPS = 1e-05

LANES = 128
BF = jnp.bfloat16
F32 = jnp.float32
OUT1 = IMG // 2
OUT2 = IMG // 4
PATCH = OUT2 // RGRID
REGIONS = RGRID * RGRID
GROUP = 8
GROUPS = OUT1 // GROUP
SEG = 21
VMEM_ALL = pl.BlockSpec(memory_space=pltpu.VMEM)


def pack_table():
    table = np.zeros((3 * LANES, GROUPS * LANES), np.float32)
    for group in range(GROUPS):
        for row in range(2):
            for ch in range(3):
                for pos in range(2 * GROUP + 1):
                    pixel = 2 * GROUP * group - 1 + pos
                    if 0 <= pixel < IMG:
                        source = ch * LANES + row * IMG + pixel
                        table[source, group * LANES + row * IMG + ch * SEG + pos] = 1.0
    return table


def tap_table():
    table = np.zeros((GROUP, 2 * LANES, 27), np.float32)
    for column in range(GROUP):
        for dy in range(3):
            base = {1: 0, 2: IMG, 0: LANES + IMG}[dy]
            for dx in range(3):
                for ch in range(3):
                    lane = base + ch * SEG + 2 * column + dx
                    table[column, lane, dy * 9 + dx * 3 + ch] = 1.0
    return table.reshape(GROUP * 2 * LANES, 27)


def camera_kernel(
    x_hbm, pack_hbm, tap_hbm, w1_hbm, w2_hbm, wt_hbm, vis_hbm, count_hbm, region_hbm, slot_hbm,
    out_ref, x_ref, pack_ref, tap_ref, w1_ref, w2_ref, wt_ref, vis_ref, count_ref, region_ref,
    slot_ref, sems, packed, wide, cells, part, *, subjects, parts, first
):
    frames_here = x_ref.shape[1]
    here = slice(first, first + frames_here)
    images_hbm = x_hbm.at[:, pl.ds(first, frames_here), :]
    sources = (
        slot_hbm, vis_hbm, count_hbm, region_hbm, w1_hbm, tap_hbm, pack_hbm, images_hbm, w2_hbm,
        wt_hbm,
    )
    targets = (
        slot_ref, vis_ref, count_ref, region_ref, w1_ref, tap_ref, pack_ref, x_ref, w2_ref, wt_ref
    )
    copies = [
        pltpu.make_async_copy(source, target, sems.at[k])
        for k, (source, target) in enumerate(zip(sources, targets))
    ]
    for copy in copies:
        copy.start()
    rows = OUT1 * frames_here
    for copy in copies[:6]:
        copy.wait()
    for column in range(GROUP):
        wide[:, column * LANES : (column + 1) * LANES] = jnp.dot(
            tap_ref[column * 2 * LANES : (column + 1) * 2 * LANES, :],
            w1_ref[...],
            preferred_element_type=F32,
        ).astype(BF)

    cells[0] = jnp.zeros(cells.shape[1:], BF)
    cells[:, 1, 0] = jnp.zeros((cells.shape[0],) + cells.shape[3:], BF)
    packed[0:frames_here, :] = jnp.zeros((frames_here, GROUPS * LANES), BF)
    copies[6].wait()
    copies[7].wait()
    images = jnp.concatenate(
        [
            jnp.concatenate(
                [x_ref[ch, :, y * LANES : (y + 1) * LANES] for ch in range(3)], axis=1
            )
            for y in range(OUT1)
        ],
        axis=0,
    )
    packed[frames_here:, :] = jnp.dot(images, pack_ref[...], preferred_element_type=F32).astype(BF)
    for group in range(GROUPS):
        lanes = slice(group * LANES, (group + 1) * LANES)
        lhs = jnp.concatenate([packed[frames_here:, lanes], packed[0:rows, lanes]], axis=1)
        for pair in range(GROUP // 2):
            both = jnp.dot(
                lhs, wide[:, pair * 2 * LANES : (pair + 1) * 2 * LANES], preferred_element_type=F32
            )
            both = jnp.maximum(both, 0.0).astype(BF)
            at = group * (GROUP // 2) + pair
            cells[1:, 0, at] = both[:, :LANES].reshape(OUT1, frames_here, LANES)
            cells[1:, 1, at + 1] = both[:, LANES:].reshape(OUT1, frames_here, LANES)

    listed = vis_ref.shape[0]
    lanes = listed * parts
    expand = (
        lax.broadcasted_iota(jnp.int32, (lanes, listed), 0) // parts
        == lax.broadcasted_iota(jnp.int32, (lanes, listed), 1)
    ).astype(BF)
    part_of = lax.broadcasted_iota(jnp.int32, (lanes, frames_here), 0) % parts
    count = jnp.dot(
        expand, count_ref[:, 0, here].astype(F32).astype(BF), preferred_element_type=F32
    ).astype(jnp.int32)
    code = jnp.where(part_of < count, region_ref[:, here] + 1, 0)
    who = vis_ref[:, 0, here]
    row_of = jnp.zeros((listed, frames_here), jnp.int32)
    for subject in range(subjects):
        row_of = jnp.where(who == subject, slot_ref[subject], row_of)
    blocks = (out_ref.shape[0] // frames_here) - REGIONS
    base = REGIONS * frames_here
    fill = jnp.zeros((blocks * LANES - lanes - listed, frames_here), F32)
    lists = jnp.concatenate([code.astype(F32), row_of.astype(F32), fill], axis=0).T.astype(BF)
    for block in range(blocks):
        out_ref[base + block * frames_here : base + (block + 1) * frames_here, :] = lists[
            :, block * LANES : (block + 1) * LANES
        ]

    copies[8].wait()
    copies[9].wait()
    width = w2_ref.shape[1]
    for ry in range(RGRID):
        total = jnp.zeros((RGRID, frames_here, width), F32)
        for y in range(ry * PATCH, (ry + 1) * PATCH):
            taps = []
            for dy in range(3):
                for parity, start in ((1, 0), (0, 0), (1, 1)):
                    taps.append(
                        cells[2 * y + dy, parity, start : start + OUT2].reshape(
                            OUT2 * frames_here, LANES
                        )
                    )
            two = jnp.dot(
                jnp.concatenate(taps, axis=1), w2_ref[...], preferred_element_type=F32
            )
            two = jnp.maximum(two, 0.0).reshape(RGRID, PATCH, frames_here, width)
            for k in range(PATCH):
                total = total + two[:, k]
        pooled = (total * (1.0 / (PATCH * PATCH))).astype(BF)
        tiles = jnp.dot(
            pooled.reshape(RGRID * frames_here, width), wt_ref[...], preferred_element_type=F32
        )
        for rx in range(RGRID):
            part[pl.ds(ry * RGRID + rx, frames_here, stride=REGIONS), :] = tiles[
                rx * frames_here : (rx + 1) * frames_here
            ]
    out_ref[0:base, :] = part[...].astype(BF)


def camera_tiles(
    frames, conv1_w, conv2_w, tile_w, vis_subject, part_count, part_region, slots, first, amount
):
    frames_here = frames.shape[1]
    listed, parts = part_region.shape[2:]
    blocks = -(-listed * (parts + 1) // LANES)
    operands = (
        jnp.transpose(frames[0], (1, 0, 2)),
        jnp.asarray(pack_table(), BF),
        jnp.asarray(tap_table(), BF),
        conv1_w,
        conv2_w,
        tile_w,
        jnp.transpose(vis_subject, (2, 0, 1)),
        jnp.transpose(part_count, (2, 0, 1)),
        jnp.transpose(part_region[0], (1, 2, 0)).reshape(listed * parts, frames_here),
        slots,
    )
    return pl.pallas_call(
        functools.partial(
            camera_kernel, subjects=slots.shape[0], parts=parts, first=first
        ),
        out_shape=jax.ShapeDtypeStruct(((REGIONS + blocks) * amount, LANES), BF),
        in_specs=[pl.BlockSpec(memory_space=pltpu.HBM)] * len(operands),
        out_specs=VMEM_ALL,
        scratch_shapes=[pltpu.VMEM((3, amount, operands[0].shape[2]), BF)]
        + [pltpu.VMEM(array.shape, array.dtype) for array in operands[1:-1]]
        + [
            pltpu.SMEM(slots.shape, slots.dtype),
            pltpu.SemaphoreType.DMA((len(operands),)),
            pltpu.VMEM(((OUT1 + 1) * amount, GROUPS * LANES), BF),
            pltpu.VMEM((2 * LANES, GROUP * LANES), BF),
            pltpu.VMEM((OUT1 + 1, 2, OUT2 + 1, amount, LANES), BF),
            pltpu.VMEM((REGIONS * amount, LANES), F32),
        ],
        cost_estimate=pl.CostEstimate(
            flops=amount * 400_000_000, bytes_accessed=amount * 100_000, transcendentals=0
        ),
        compiler_params=pltpu.CompilerParams(vmem_limit_bytes=60 << 20),
    )(*operands)


def exchange(chunks):
    cams = lax.axis_size("cam")
    if cams & (cams - 1):
        gathered = [lax.all_gather(chunk, "cam", axis=0, tiled=False) for chunk in chunks]
        return [[whole[c] for c in range(cams)] for whole in gathered]

    def swap(array, bits):
        return lax.ppermute(array, "cam", [(i, i ^ bits) for i in range(cams)])

    results = []
    for chunk in chunks:
        far = [chunk]
        for bits in [1 << k for k in reversed(range(3, cams.bit_length() - 1))]:
            far = far + [swap(piece, bits) for piece in far]
        beside = [swap(chunk, 2)] + [swap(piece, 2) for piece in far[1:]]
        near = [swap(piece, 4) for piece in far]
        both = far + beside + near + [swap(near[0], 2)] + [swap(piece, 4) for piece in beside[1:]]
        results.append(both + [swap(piece, 1) for piece in both])
    return results


def token_kernel(*refs, cams, parts, listed, amounts):
    count = cams * len(amounts)
    tokens_ref, normed_ref = refs[count : count + 2]
    own = refs[count + 2 : count + 2 + len(amounts)]
    sems, marks, spots, picks, summed = refs[count + 2 + len(amounts) :]
    copies = [
        pltpu.make_async_copy(refs[k * cams], own[k], sems.at[k]) for k in range(len(amounts))
    ]
    for copy in copies:
        copy.start()
    places = SUBJ_DEV * parts
    mine = lax.axis_index("cam") * SUBJ_DEV
    blocks = own[0].shape[0] // amounts[0] - REGIONS
    lanes = blocks * LANES
    from_lane = lax.broadcasted_iota(jnp.int32, (SUBJ_DEV * lanes, LANES), 0)
    to_lane = lax.broadcasted_iota(jnp.int32, (SUBJ_DEV * lanes, LANES), 1)
    fold = (
        (from_lane % parts == to_lane % parts) & (from_lane // lanes == to_lane // parts)
    ).astype(BF)
    views = listed * parts
    from_view = lax.broadcasted_iota(jnp.int32, (lanes, lanes), 0)
    to_view = lax.broadcasted_iota(jnp.int32, (lanes, lanes), 1)
    repeat = ((from_view == views + to_view // parts) & (to_view < views)).astype(BF)
    widen = (
        lax.broadcasted_iota(jnp.int32, (cams, cams * REGIONS), 1) // REGIONS
        == lax.broadcasted_iota(jnp.int32, (cams, cams * REGIONS), 0)
    ).astype(BF)
    ahead = 0
    for k, amount in enumerate(amounts):
        pieces = (own[k],) + refs[k * cams + 1 : (k + 1) * cams]
        copies[k].wait()
        base = REGIONS * amount
        lists = jnp.concatenate(
            [
                jnp.concatenate(
                    [
                        piece[base + b * amount : base + (b + 1) * amount, :]
                        for b in range(blocks)
                    ],
                    axis=1,
                )
                for piece in pieces
            ],
            axis=0,
        )
        row = jnp.dot(lists, repeat, preferred_element_type=F32)
        lane = lax.broadcasted_iota(jnp.int32, row.shape, 1)
        code = jnp.where(lane < views, lists.astype(F32), 0.0)
        codes = [
            jnp.where(row == (mine + s).astype(F32), code, 0.0).astype(BF) for s in range(SUBJ_DEV)
        ]
        marks[0 : cams * amount, :] = jnp.dot(
            jnp.concatenate(codes, axis=1), fold, preferred_element_type=F32
        )
        for f in range(amount):
            found = marks[pl.ds(f, cams, stride=amount), :]
            spots[f * places : (f + 1) * places, :] = found.T[:places].astype(BF)
        spread = jnp.dot(
            spots[0 : amount * places, :], widen, preferred_element_type=F32
        )
        region = lax.broadcasted_iota(jnp.int32, spread.shape, 1) % REGIONS + 1
        picks[0 : amount * places, :] = jnp.where(spread == region.astype(F32), 1.0, 0.0).astype(BF)
        for f in range(amount):
            tiles = jnp.concatenate(
                [piece[f * REGIONS : (f + 1) * REGIONS, :] for piece in pieces], axis=0
            )
            summed[(ahead + f) * places : (ahead + f + 1) * places, :] = jnp.dot(
                picks[f * places : (f + 1) * places, :], tiles, preferred_element_type=F32
            )
        ahead += amount
    for s in range(SUBJ_DEV):
        tokens = jnp.concatenate(
            [summed[pl.ds(s * parts + p, ahead, stride=places), :] for p in range(parts)],
            axis=1,
        )
        tokens_ref[s * ahead : (s + 1) * ahead, :] = tokens
        power = jnp.mean(tokens * tokens, axis=1, keepdims=True)
        normed_ref[s * ahead : (s + 1) * ahead, :] = (tokens * lax.rsqrt(power + EPS)).astype(BF)


def build_tokens(gathered, parts, listed, amounts):
    cams = len(gathered[0])
    frames_here, most = sum(amounts), max(amounts)
    rows = SUBJ_DEV * frames_here
    width = parts * LANES
    places = SUBJ_DEV * parts
    return pl.pallas_call(
        functools.partial(
            token_kernel, cams=cams, parts=parts, listed=listed, amounts=amounts
        ),
        out_shape=(
            jax.ShapeDtypeStruct((rows, width), F32),
            jax.ShapeDtypeStruct((rows, width), BF),
        ),
        in_specs=([pl.BlockSpec(memory_space=pl.ANY)] + [VMEM_ALL] * (cams - 1)) * len(amounts),
        out_specs=(VMEM_ALL, VMEM_ALL),
        scratch_shapes=[pltpu.VMEM(pieces[0].shape, BF) for pieces in gathered]
        + [
            pltpu.SemaphoreType.DMA((len(amounts),)),
            pltpu.VMEM((cams * most, LANES), F32),
            pltpu.VMEM((most * places, cams), BF),
            pltpu.VMEM((most * places, cams * REGIONS), BF),
            pltpu.VMEM((frames_here * places, LANES), F32),
        ],
        compiler_params=pltpu.CompilerParams(vmem_limit_bytes=10 << 20),
    )(*[piece for pieces in gathered for piece in pieces])


def project_kernel(
    normed_ref, qkv_w_hbm, mixed_ref, key_w_ref, value_w_ref, query_w_ref, sems
):
    width = normed_ref.shape[1]
    half = width // 2
    targets = (query_w_ref, key_w_ref, value_w_ref)
    pieces = [(target, k, at) for k, target in enumerate(targets) for at in (0, half)]
    copies = [
        pltpu.make_async_copy(
            qkv_w_hbm.at[:, pl.ds(k * width + at, half)], target.at[:, pl.ds(at, half)], sems.at[n]
        )
        for n, (target, k, at) in enumerate(pieces)
    ]
    for copy in copies:
        copy.start()
    for copy, (target, k, at) in zip(copies, pieces):
        copy.wait()
        mixed_ref[:, k * width + at : k * width + at + half] = jnp.dot(
            normed_ref[...], target[:, at : at + half], preferred_element_type=F32
        ).astype(BF)


def project(normed, qkv_w):
    rows, width = normed.shape
    hbm = pl.BlockSpec(memory_space=pltpu.HBM)
    square = jax.ShapeDtypeStruct((width, width), BF)
    return pl.pallas_call(
        project_kernel,
        out_shape=[jax.ShapeDtypeStruct((rows, 3 * width), BF), square, square],
        in_specs=[VMEM_ALL, hbm],
        out_specs=[VMEM_ALL] * 3,
        scratch_shapes=[pltpu.VMEM((width, width), BF), pltpu.SemaphoreType.DMA((6,))],
        cost_estimate=pl.CostEstimate(
            flops=2 * rows * width * 3 * width,
            bytes_accessed=2 * qkv_w.size,
            transcendentals=0,
        ),
        compiler_params=pltpu.CompilerParams(vmem_limit_bytes=47 << 20),
    )(normed, qkv_w)


def attention_kernel(
    mixed_ref, other_ref, key_w_ref, value_w_ref, tokens_ref, out_w_hbm, bias_hbm,
    out_ref, out_w_ref, bias_ref, sems, other_keys, other_values, scores, weights, totals, attended, *, frames_here
):
    rows, width = tokens_ref.shape
    others = other_ref.shape[0] // rows
    head_size = width // HEADS
    scale = 1.0 / math.sqrt(head_size)
    splits = others + 1
    span = splits * frames_here
    heads = LANES // head_size
    block = heads * frames_here
    tiles = width // LANES
    head_of = lax.broadcasted_iota(jnp.int32, (frames_here, LANES), 1) // head_size
    place = lax.axis_index("frame")
    copies = [
        pltpu.make_async_copy(source, target, sems.at[k])
        for k, (source, target) in enumerate(((bias_hbm, bias_ref), (out_w_hbm, out_w_ref)))
    ]
    for copy in copies:
        copy.start()
    other_keys[...] = jnp.dot(
        other_ref[...], key_w_ref[...], preferred_element_type=F32
    ).astype(BF)
    other_values[...] = jnp.dot(
        other_ref[...], value_w_ref[...], preferred_element_type=F32
    ).astype(BF)

    def gathered(n, tile, own, rest):
        at = n * frames_here
        return jnp.concatenate(
            [mixed_ref[at : at + frames_here, own + tile * LANES : own + (tile + 1) * LANES]]
            + [
                rest[k * rows + at : k * rows + at + frames_here, tile * LANES : (tile + 1) * LANES]
                for k in range(others)
            ],
            axis=0,
        )

    copies[0].wait()
    for n in range(SUBJ_DEV):
        bias = bias_ref[n]
        turned = bias
        for k in range(1, splits):
            turn = jnp.concatenate(
                [bias[:, k * frames_here :], bias[:, : k * frames_here]], axis=1
            )
            turned = jnp.where(place == k, turn, turned)
        for tile in range(tiles):
            query = mixed_ref[
                n * frames_here : (n + 1) * frames_here, tile * LANES : (tile + 1) * LANES
            ]
            queries = jnp.concatenate(
                [jnp.where(head_of == h, query, jnp.zeros((), BF)) for h in range(heads)], axis=0
            )
            products = lax.dot_general(
                queries,
                gathered(n, tile, width, other_keys),
                (((1,), (1,)), ((), ())),
                preferred_element_type=F32,
            )
            added = jnp.concatenate(
                [
                    jnp.broadcast_to(
                        turned[tile * heads + h : tile * heads + h + 1, :], (frames_here, span)
                    )
                    for h in range(heads)
                ],
                axis=0,
            )
            at = (n * tiles + tile) * block
            scores[at : at + block, :] = products * scale + added
    for n in range(SUBJ_DEV):
        part = slice(n * tiles * block, (n + 1) * tiles * block)
        raw = scores[part, :]
        raised = jnp.exp(raw - jnp.max(raw, axis=1, keepdims=True))
        weights[part, :] = raised.astype(BF)
        totals[part, :] = jnp.broadcast_to(
            jnp.sum(raised, axis=1, keepdims=True), (tiles * block, LANES)
        )
    for n in range(SUBJ_DEV):
        for tile in range(tiles):
            at = (n * tiles + tile) * block
            ratio = (
                jnp.dot(
                    weights[at : at + block, :],
                    gathered(n, tile, 2 * width, other_values),
                    preferred_element_type=F32,
                )
                / totals[at : at + block, :]
            )
            result = ratio[:frames_here]
            for h in range(1, heads):
                result = jnp.where(
                    head_of == h, ratio[h * frames_here : (h + 1) * frames_here], result
                )
            attended[
                n * frames_here : (n + 1) * frames_here, tile * LANES : (tile + 1) * LANES
            ] = result.astype(BF)
    copies[1].wait()
    out_ref[...] = (
        tokens_ref[...] + jnp.dot(attended[...], out_w_ref[...], preferred_element_type=F32)
    ).astype(BF)


def attend(mixed, other, key_w, value_w, out_w, bias, tokens, frames_here):
    rows, width = tokens.shape
    span = bias.shape[2]
    return pl.pallas_call(
        functools.partial(attention_kernel, frames_here=frames_here),
        out_shape=jax.ShapeDtypeStruct((rows, width), BF),
        in_specs=[VMEM_ALL] * 5 + [pl.BlockSpec(memory_space=pltpu.HBM)] * 2,
        out_specs=VMEM_ALL,
        scratch_shapes=[
            pltpu.VMEM(out_w.shape, BF),
            pltpu.VMEM(bias.shape, F32),
            pltpu.SemaphoreType.DMA((2,)),
            pltpu.VMEM(other.shape, BF),
            pltpu.VMEM(other.shape, BF),
            pltpu.VMEM((HEADS * rows, span), F32),
            pltpu.VMEM((HEADS * rows, span), BF),
            pltpu.VMEM((HEADS * rows, LANES), F32),
            pltpu.VMEM((rows, width), BF),
        ],
        compiler_params=pltpu.CompilerParams(vmem_limit_bytes=14 << 20),
    )(mixed, other, key_w, value_w, tokens, out_w, bias)


def per_device(
    frames, conv1_w, conv2_w, tile_w, vis_subject, part_count, part_region, subject_slot,
    qkv_w, out_w, key_bias
):
    frames_here = frames.shape[1]
    parts = part_region.shape[3]
    amounts = (frames_here // 2, frames_here // 2) if frames_here % 32 == 77 else (frames_here,)
    chunks = [
        camera_tiles(
            frames, conv1_w, conv2_w, tile_w, vis_subject, part_count, part_region, subject_slot,
            sum(amounts[:k]), amount,
        )
        for k, amount in enumerate(amounts)
    ]
    tokens, normed = build_tokens(exchange(chunks), parts, part_region.shape[2], amounts)
    splits = lax.axis_size("frame")
    others = [
        lax.ppermute(normed, "frame", [((i + k) % splits, i) for i in range(splits)])
        for k in range(1, splits)
    ]
    other = others[0] if splits == 2 else jnp.concatenate(others, axis=0)
    mixed, key_w, value_w = project(normed, qkv_w)
    posed = attend(mixed, other, key_w, value_w, out_w, key_bias, tokens, frames_here)
    return posed.reshape(SUBJ_DEV, frames_here, tokens.shape[1])


def solution(mesh):
    in_specs = (
        P("cam", "frame", None, None),
        P(),
        P(),
        P(),
        P("cam", "frame", None),
        P("cam", "frame", None),
        P("cam", "frame", None, None),
        P(),
        P(),
        P(),
        P("cam", None, None),
    )
    out_specs = P("cam", "frame", None)
    return jax.shard_map(
        per_device, mesh=mesh, in_specs=in_specs, out_specs=out_specs, check_vma=False
    )
```
